32 devices in a mesh: box: 8 (over z, x), dir: 4 (over y, core).
Axes of the slice: x: 2, y: 2, z: 4, core: 2. Of those that a mesh axis runs over, the one named last changes fastest.
Arguments:
- leaf_patterns: float32 [16, 16, 2, 64, 128], P('box', 'dir'), may hold values from -6 to 6
- occupancy: int32 [16], P('box'), may hold values from 0 to 16
- pair_lists: int32 [4, 1, 4], replicated, may hold values from 0 to 2, as said below
Outputs:
- translated: float32 [8, 1, 16, 2, 128, 512], P('box', None, None, None, 'dir')
The draws below stay inside these ranges and needn't reach their ends.
Inputs may be any that keep to these rules, and one draw needn't show every extreme that they name: `pair_lists`: each box's list names 4 source boxes, repeats allowed: positions 0 to 0 are the boxes of the pair before its own, 1 to 1 its own pair, the rest the pair after; never the box itself and never a pair outside 0 .. 3.
All inputs are finite; a program needn't handle non-finite values.
Results may differ from the reference program's by a relative error of at most 0.0003.
Values sent between devices are 32-bit elements; how exact they have to be, the bound alone decides.
A program may use at most 64 MiB of HBM per device.

```python
import jax
import jax.numpy as jnp
from jax import lax

LT = 64
LP = 128
RHS = 16
K = 4
LTR = 16
SLOTS = 1
N_LEAF = 16
PAIRS = 4
N_BOX = 8


def draw_leaf_patterns(key, part):
    noise_key, level_key = jax.random.split(key, 2)
    parity = (1 - 2 * (jnp.arange(LP, dtype=jnp.int32) % 2)).astype(jnp.float32)
    noise_part = 0.8 * jnp.clip(jax.random.normal(noise_key, (N_LEAF, RHS, 2, LT, LP), jnp.float32), -4.0, 4.0)
    level_part = jax.random.normal(level_key, (N_LEAF, RHS, 2, LT, 1), jnp.float32)
    return jnp.clip(noise_part + level_part * parity, -6.0, 6.0).astype(jnp.float32)


def draw_pair_lists(key, part):
    pair_numbers = jnp.arange(PAIRS, dtype=jnp.int32)[:, None, None]
    slot_numbers = jnp.arange(SLOTS, dtype=jnp.int32)[None, :, None]
    lowest = jnp.where(pair_numbers > 0, 0, SLOTS)
    highest_end = jnp.where(pair_numbers < PAIRS - 1, 3 * SLOTS, 2 * SLOTS)
    spread = highest_end - lowest - 1
    random_bits = jax.random.randint(key, (PAIRS, SLOTS, K), 0, 1 << 20, dtype=jnp.int32)
    chosen = lowest + random_bits % spread
    chosen = jnp.where(chosen >= SLOTS + slot_numbers, chosen + 1, chosen)
    chosen = chosen.at[1, 0, 0].set(3 * SLOTS - 1)
    chosen = chosen.at[1, 0, 1].set(0)
    return chosen.astype(jnp.int32)


def plant(drawn, key, smallest, high):
    longest = drawn.shape.index(max(drawn.shape))
    spots = []
    for shift in (0, 1):
        where = [jax.random.randint(jax.random.fold_in(key, axis), (), 0, length) for axis, length in enumerate(drawn.shape)]
        where[longest] = (where[longest] + shift) % drawn.shape[longest]
        spots.append(tuple(where))
    return drawn.at[spots[0]].set(smallest).at[spots[1]].set(high)


def setup_inputs(seed: int = 0) -> dict:
    key_list = jax.random.split(jax.random.key(seed), 4)
    return {
        "leaf_patterns": draw_leaf_patterns(jax.random.fold_in(key_list[3], 71), 0),
        "occupancy": plant(jax.random.randint(key_list[1], (N_LEAF,), 0, 17), jax.random.fold_in(key_list[1], 1), 0, 16).astype(jnp.int32),
        "pair_lists": draw_pair_lists(jax.random.fold_in(key_list[3], 71), 0),
    }


full_count = 16.0
phase_first = 16.0
phase_second = 64.0
translate_wave = 20.0
highest = lax.Precision.HIGHEST

def interp_table(points, offset):
    mode_count = points // 2
    orders = jnp.arange(mode_count + 1, dtype=jnp.float32)
    weights = jnp.where((orders == 0) | (orders == mode_count), 1.0, 2.0) / points
    source = (jnp.arange(points, dtype=jnp.float32) + offset) / points
    target = (jnp.arange(2 * points, dtype=jnp.float32) + offset) / (2 * points)
    source_angle = 2.0 * jnp.pi * source[:, None] * orders[None, :]
    target_angle = 2.0 * jnp.pi * target[:, None] * orders[None, :]
    return jnp.dot(jnp.cos(target_angle) * weights, jnp.cos(source_angle).T, precision=highest) + jnp.dot(jnp.sin(target_angle) * weights, jnp.sin(source_angle).T, precision=highest)

def directions(row_numbers, rows_total, columns):
    theta_rows = (jnp.pi * (row_numbers.astype(jnp.float32) + 0.5) / rows_total)[:, None]
    azimuth = 2.0 * jnp.pi / columns * jnp.arange(columns, dtype=jnp.float32)[None, :]
    sine_theta = jnp.sin(theta_rows)
    return (sine_theta * jnp.cos(azimuth), sine_theta * jnp.sin(azimuth), jnp.cos(theta_rows) * jnp.ones_like(azimuth))

def interpolate(pattern, row_table, column_table):
    rows_done = jnp.einsum('it,...tp->...ip', row_table, pattern, precision=highest)
    return jnp.einsum('...ip,qp->...iq', rows_done, column_table, precision=highest)

def apply_phase(pattern, angles):
    real_part = pattern[..., 0, :, :]
    imag_part = pattern[..., 1, :, :]
    cosine = jnp.cos(angles)
    sine_value = jnp.sin(angles)
    return jnp.stack([real_part * cosine - imag_part * sine_value, real_part * sine_value + imag_part * cosine], axis=-3)

def contribute(child_pattern, child_sign, row_start, row_count, row_table, column_table, wave_scale, component):
    rows_used = lax.dynamic_slice_in_dim(row_table, row_start, row_count, 0)
    row_numbers = row_start + jnp.arange(row_count, dtype=jnp.int32)
    along_x, along_y, along_z = directions(row_numbers, row_table.shape[0], column_table.shape[0])
    picked_axis = along_x if component == 0 else along_y
    angles = picked_axis * (wave_scale * child_sign)
    return apply_phase(interpolate(child_pattern, rows_used, column_table), angles)

def box_center(numbers):
    return jnp.stack([numbers % 4, numbers // 4 % 4, numbers // 16], axis=-1).astype(jnp.float32)

def translation_table(offsets, along_x, along_y, along_z):
    distance = jnp.sqrt(lax.optimization_barrier(jnp.sum(offsets * offsets, axis=1)))
    unit_vector = offsets / distance[:, None]
    cosine = unit_vector[:, 0, None, None] * along_x[None] + unit_vector[:, 1, None, None] * along_y[None] + unit_vector[:, 2, None, None] * along_z[None]
    argument = (translate_wave * distance)[:, None, None]
    sine_arg = jnp.sin(argument)
    cosine_arg = jnp.cos(argument)
    squared = argument * argument
    hankel_now = (sine_arg / argument, -cosine_arg / argument)
    hankel_next = ((sine_arg - argument * cosine_arg) / squared, -(argument * sine_arg + cosine_arg) / squared)
    legendre_now = jnp.ones_like(cosine)
    legendre_next = cosine
    summed_real = jnp.zeros_like(cosine)
    summed_imag = jnp.zeros_like(cosine)
    for degree in range(LTR + 1):
        weight_now = (2.0 * degree + 1.0) * legendre_now
        real_now, imag_now = hankel_now
        if degree % 4 == 0:
            turned = (real_now, imag_now)
        elif degree % 4 == 1:
            turned = (-imag_now, real_now)
        elif degree % 4 == 2:
            turned = (-real_now, -imag_now)
        else:
            turned = (imag_now, -real_now)
        summed_real = summed_real + weight_now * turned[0]
        summed_imag = summed_imag + weight_now * turned[1]
        factor = (2.0 * degree + 3.0) / argument
        hankel_now, hankel_next = (hankel_next, (factor * hankel_next[0] - hankel_now[0], factor * hankel_next[1] - hankel_now[1]))
        legendre_now, legendre_next = (legendre_next, ((2.0 * degree + 3.0) * cosine * legendre_next - (degree + 1.0) * legendre_now) / (degree + 2.0))
    return jnp.stack([summed_real, summed_imag], axis=1) / offsets.shape[0]

def complex_sum(operator_table, picked):
    table_real = operator_table[:, 0][:, None]
    table_imag = operator_table[:, 1][:, None]
    source_real = picked[:, :, 0]
    source_imag = picked[:, :, 1]
    return jnp.stack([lax.optimization_barrier(jnp.sum(table_real * source_real - table_imag * source_imag, axis=0)), lax.optimization_barrier(jnp.sum(table_real * source_imag + table_imag * source_real, axis=0))], axis=1)

def reference(leaf_patterns, occupancy, pair_lists):
    weighted = leaf_patterns * (occupancy.astype(jnp.float32) / full_count)[:, None, None, None, None]
    first_rows = interp_table(LT, 0.5)
    first_columns = interp_table(LP, 0.0)
    second_rows = interp_table(2 * LT, 0.5)
    second_columns = interp_table(2 * LP, 0.0)

    def merge_first(number):
        pair_leaves = lax.dynamic_slice_in_dim(weighted, 2 * number, 2, 0)
        summed = contribute(pair_leaves[0], -1.0, 0, 2 * LT, first_rows, first_columns, phase_first, 0)
        return summed + contribute(pair_leaves[1], 1.0, 0, 2 * LT, first_rows, first_columns, phase_first, 0)
    first_level = lax.map(merge_first, jnp.arange(N_LEAF // 2, dtype=jnp.int32))

    def merge_second(number):
        pair_id = number // SLOTS
        slot_id = number % SLOTS
        lower_child = lax.dynamic_index_in_dim(first_level, 2 * pair_id * SLOTS + slot_id, 0, keepdims=False)
        upper_child = lax.dynamic_index_in_dim(first_level, (2 * pair_id + 1) * SLOTS + slot_id, 0, keepdims=False)
        summed = contribute(lower_child, -1.0, 0, 4 * LT, second_rows, second_columns, phase_second, 1)
        return summed + contribute(upper_child, 1.0, 0, 4 * LT, second_rows, second_columns, phase_second, 1)
    second_level = lax.map(merge_second, jnp.arange(PAIRS * SLOTS, dtype=jnp.int32))
    along_x, along_y, along_z = directions(jnp.arange(4 * LT, dtype=jnp.int32), 4 * LT, 4 * LP)

    def translate(number):
        pair_id = number // SLOTS
        slot_id = number % SLOTS
        chosen = pair_lists[pair_id, slot_id]
        source_ids = pair_id * SLOTS - SLOTS + chosen
        offsets = box_center(number)[None, :] - box_center(source_ids)
        operator_table = translation_table(offsets, along_x, along_y, along_z)
        picked = jnp.take(second_level, source_ids, axis=0)
        return complex_sum(operator_table, picked)
    incoming = lax.map(translate, jnp.arange(PAIRS * SLOTS, dtype=jnp.int32))
    shaped = incoming.reshape(PAIRS, SLOTS, RHS, 2, 2, 2 * LT, 4 * LP).transpose(0, 4, 1, 2, 3, 5, 6)
    return shaped.reshape(N_BOX, SLOTS, RHS, 2, 2 * LT, 4 * LP)
```

```python
import functools

import jax
import jax.numpy as jnp
import numpy as np
from jax import lax
from jax.experimental import pallas as pl
from jax.experimental.pallas import tpu as pltpu
from jax.sharding import PartitionSpec as P

MESH = pl.DeviceIdType.MESH
LTR = 16
full_count = 16.0
phase_first = 16.0
phase_second = 64.0
translate_wave = 20.0


def interp_table(points, offset):
    orders = np.arange(points // 2 + 1, dtype=np.float64)
    weights = np.where((orders == 0) | (orders == points // 2), 1.0, 2.0) / points
    source = (np.arange(points) + offset) / points
    target = (np.arange(2 * points) + offset) / (2 * points)
    angle = 2.0 * np.pi * (target[:, None, None] - source[None, :, None]) * orders
    return (np.cos(angle) * weights).sum(-1)


def halves(table):
    high = np.asarray(table, np.float32).astype(jnp.bfloat16)
    low = (np.asarray(table, np.float64) - high.astype(np.float64)).astype(jnp.bfloat16)
    return high, low


def sines(rows, columns):
    theta = np.pi * (np.arange(rows) + 0.5) / rows
    phi = 2.0 * np.pi * np.arange(columns) / columns
    return np.sin(theta), np.cos(theta), np.cos(phi), np.sin(phi)


def center(g):
    return np.array([g % 4, g // 4 % 4, g // 16], np.float64)


def series_table(pairs):
    table = np.zeros((pairs, 2 * (3 + 2 * (LTR + 1))), np.float64)
    width = 3 + 2 * (LTR + 1)
    for g in range(pairs):
        for side, s in enumerate((g - 1, g + 1)):
            if not 0 <= s < pairs:
                continue
            r = center(g) - center(s)
            distance = np.sqrt((r * r).sum())
            x = translate_wave * distance
            now = (np.sin(x) - 1j * np.cos(x)) / x
            nxt = ((np.sin(x) - x * np.cos(x)) - 1j * (x * np.sin(x) + np.cos(x))) / x**2
            table[g, side * width : side * width + 3] = r / distance
            for degree in range(LTR + 1):
                value = (1j**degree) * (2 * degree + 1) * now
                table[g, side * width + 3 + 2 * degree] = value.real
                table[g, side * width + 4 + 2 * degree] = value.imag
                now, nxt = nxt, (2 * degree + 3) / x * nxt - now
    return table.astype(np.float32)


def split(value):
    high = value.astype(jnp.bfloat16)
    low = (value - high.astype(jnp.float32)).astype(jnp.bfloat16)
    return high, low


def dot(a, b):
    return jnp.dot(a, b, preferred_element_type=jnp.float32)


def kernel(
    sizes,
    leaf, occ, lists, series, c1, r1, r2, c2, ph1, ph2, polar, azim,
    out,
    mine, other, lhs1, rhs1, first, rhs2, lhs2, ready, relay, land, oper,
    xs, xr, ds, dr, zs, zr,
):
    n_box, n_dir, count, lt, lp, slab = sizes
    box = lax.axis_index("box")
    me = lax.axis_index("dir")
    half = box % 2
    pair = box // 2
    pairs = n_box // 2
    has_lower = pair > 0
    has_upper = pair < pairs - 1
    partner = box + 1 - 2 * half

    barrier = pltpu.get_barrier_semaphore()
    pl.semaphore_signal(barrier, inc=1, device_id=(partner, me), device_id_type=MESH)
    for o in range(1, n_dir):
        pl.semaphore_signal(
            barrier, inc=1, device_id=(box, (me + o) % n_dir), device_id_type=MESH
        )

    @pl.when(has_lower)
    def _():
        pl.semaphore_signal(barrier, inc=1, device_id=(box - 2, me), device_id_type=MESH)

    @pl.when(has_upper)
    def _():
        pl.semaphore_signal(barrier, inc=1, device_id=(box + 2, me), device_id_type=MESH)

    w0 = occ[0].astype(jnp.float32) / full_count
    w1 = occ[1].astype(jnp.float32) / full_count
    for r in range(count):
        for c in range(2):
            a = leaf[0, r, c] * w0
            b = leaf[1, r, c] * w1
            mine[r, c] = a + b
            mine[r, 2 + c] = b - a

    pl.semaphore_wait(
        barrier, n_dir + has_lower.astype(jnp.int32) + has_upper.astype(jnp.int32)
    )

    def x_copy(r):
        return pltpu.make_async_remote_copy(
            mine.at[r], other.at[r], xs.at[r], xr.at[r], (partner, me), device_id_type=MESH
        )

    for r in range(count):
        x_copy(r).start()

    def d_copy(r, o):
        peer = (me + o) % n_dir
        return pltpu.make_async_remote_copy(
            ready.at[r, peer], relay.at[me, r], ds.at[r, o], dr.at[r, n_dir - o],
            (box, peer), device_id_type=MESH,
        )

    def d_arrival(r, o):
        peer = (me + o) % n_dir
        return pltpu.make_async_remote_copy(
            ready.at[r, me], relay.at[peer, r], ds.at[r, o], dr.at[r, o],
            (box, peer), device_id_type=MESH,
        )

    def z_copy(r, o, up):
        source = (me + o) % n_dir
        chunk = ready.at[r, me] if o == 0 else relay.at[source, r]
        side = 0 if up else 1
        return pltpu.make_async_remote_copy(
            chunk, land.at[side, source, r], zs.at[side, r, o], zr.at[side, r, o],
            (box + 2 if up else box - 2, me), device_id_type=MESH,
        )

    def z_start(r, o):
        @pl.when(has_upper)
        def _():
            z_copy(r, o, True).start()

        @pl.when(has_lower)
        def _():
            z_copy(r, o, False).start()

    for side, present in ((0, has_lower), (1, has_upper)):
        @pl.when(jnp.logical_not(present))
        def _():
            land[side] = jnp.zeros(land.shape[1:], jnp.float32)

    def first_level(source, r):
        for k in range(4):
            high, low = split(source[r, k])
            rows = pl.ds(k * lt, lt)
            lhs1[rows, 0:lp] = high
            lhs1[rows, lp : 2 * lp] = low
            lhs1[rows, 2 * lp : 3 * lp] = high
        wide = dot(lhs1[...], c1[...])
        for k in range(4):
            high, low = split(wide[k * lt : (k + 1) * lt])
            columns = pl.ds(k * 2 * lp, 2 * lp)
            rhs1[0:lt, columns] = high
            rhs1[lt : 2 * lt, columns] = low
            rhs1[2 * lt : 3 * lt, columns] = high
        sr, si, dre, dim = [
            dot(r1[...], rhs1[:, k * 2 * lp : (k + 1) * 2 * lp]) for k in range(4)
        ]
        cosine, sine = ph1[0], ph1[1]
        return cosine * sr - sine * dim, cosine * si + sine * dre

    sign = (2 * half - 1).astype(jnp.float32)
    row_start = pl.multiple_of(half * 2 * lt, 2 * lt)

    def level_step(r, carry):
        fr, fi = first_level(mine, r)
        first[0] = fr
        first[1] = fi
        x_copy(r).wait_recv()
        gr, gi = first_level(other, r)
        for k, value in enumerate(
            (first[0] + gr, first[1] + gi, (first[0] - gr) * sign, (first[1] - gi) * sign)
        ):
            high, low = split(value)
            columns = pl.ds(k * 2 * lp, 2 * lp)
            rhs2[0 : 2 * lt, columns] = high
            rhs2[2 * lt : 4 * lt, columns] = low
            rhs2[4 * lt : 6 * lt, columns] = high
        for k in range(4):
            high, low = split(dot(r2[half], rhs2[:, k * 2 * lp : (k + 1) * 2 * lp]))
            rows = pl.ds(k * 2 * lt, 2 * lt)
            lhs2[rows, 0 : 2 * lp] = high
            lhs2[rows, 2 * lp : 4 * lp] = low
            lhs2[rows, 4 * lp : 6 * lp] = high
        for d in range(n_dir):
            sr, si, dre, dim = [
                dot(lhs2[pl.ds(k * 2 * lt + d * slab, slab), :], c2[...]) for k in range(4)
            ]
            rows = pl.ds(row_start + d * slab, slab)
            cosine, sine = ph2[0, rows], ph2[1, rows]
            ready[r, d, 0] = cosine * sr - sine * dim
            ready[r, d, 1] = cosine * si + sine * dre
        z_start(r, 0)
        for o in range(1, n_dir):
            d_copy(r, o).start()

        @pl.when(r > 0)
        def _():
            for o in range(1, n_dir):
                d_arrival(r - 1, o).wait_recv()
                z_start(r - 1, o)

        return carry

    lax.fori_loop(0, count, level_step, 0)
    for o in range(1, n_dir):
        d_arrival(count - 1, o).wait_recv()
        z_start(count - 1, o)

    slots = lists.shape[1]
    entries = lists.shape[2]
    slab_rows = pl.ds(pl.multiple_of(half * 2 * lt + me * slab, slab), slab)
    sine_theta = polar[0, slab_rows]
    along_x = sine_theta * azim[0:1]
    along_y = sine_theta * azim[1:2]
    along_z = polar[1, slab_rows] * jnp.ones_like(along_x)
    width = 3 + 2 * (LTR + 1)
    for side in range(2):
        named = jnp.float32(0.0)
        for k in range(entries):
            chosen = lists[pair, 0, k]
            hit = chosen < slots if side == 0 else chosen >= 2 * slots
            named = named + jnp.where(hit, 1.0, 0.0)
        scale = named / entries
        base = side * width
        u = (
            series[pair, base] * along_x
            + series[pair, base + 1] * along_y
            + series[pair, base + 2] * along_z
        )
        now, nxt = jnp.ones_like(u), u
        real, imag = jnp.zeros_like(u), jnp.zeros_like(u)
        for degree in range(LTR + 1):
            real = real + series[pair, base + 3 + 2 * degree] * now
            imag = imag + series[pair, base + 4 + 2 * degree] * now
            now, nxt = nxt, (
                ((2.0 * degree + 3.0) / (degree + 2.0)) * (u * nxt)
                - ((degree + 1.0) / (degree + 2.0)) * now
            )
        oper[side, 0] = real * scale
        oper[side, 1] = imag * scale

    def apply_step(r, carry):
        for o in range(n_dir):
            source = (me + o) % n_dir

            @pl.when(has_lower)
            def _():
                z_copy(r, o, True).wait_recv()

            @pl.when(has_upper)
            def _():
                z_copy(r, o, False).wait_recv()

            lr, li = land[0, source, r, 0], land[0, source, r, 1]
            ur, ui = land[1, source, r, 0], land[1, source, r, 1]
            out[source, r, 0] = (
                oper[0, 0] * lr - oper[0, 1] * li + oper[1, 0] * ur - oper[1, 1] * ui
            )
            out[source, r, 1] = (
                oper[0, 0] * li + oper[0, 1] * lr + oper[1, 0] * ui + oper[1, 1] * ur
            )
        return carry

    lax.fori_loop(0, count, apply_step, 0)

    for r in range(count):
        x_copy(r).wait_send()
        for o in range(1, n_dir):
            d_copy(r, o).wait_send()
        for o in range(n_dir):
            @pl.when(has_upper)
            def _():
                z_copy(r, o, True).wait_send()

            @pl.when(has_lower)
            def _():
                z_copy(r, o, False).wait_send()


def per_device(n_box, n_dir, leaf_patterns, occupancy, pair_lists):
    _, count, _, lt, lp = leaf_patterns.shape
    assert leaf_patterns.shape[0] == 2
    slab = 2 * lt // n_dir
    bf16 = jnp.bfloat16
    first_high, first_low = halves(interp_table(lp, 0.0).T)
    c1 = np.concatenate([first_high, first_high, first_low], axis=0)
    row_high, row_low = halves(interp_table(lt, 0.5))
    r1 = np.concatenate([row_high, row_high, row_low], axis=1)
    row_high, row_low = halves(interp_table(2 * lt, 0.5).reshape(2, 2 * lt, 2 * lt))
    r2 = np.concatenate([row_high, row_high, row_low], axis=2)
    high, low = halves(interp_table(2 * lp, 0.0).T)
    c2 = np.concatenate([high, high, low], axis=0)
    st, _, cp, _ = sines(2 * lt, 2 * lp)
    angle = phase_first * st[:, None] * cp[None]
    ph1 = np.stack([np.cos(angle), np.sin(angle)]).astype(np.float32)
    st, ct, cp, sp = sines(4 * lt, 4 * lp)
    angle = phase_second * st[:, None] * sp[None]
    ph2 = np.stack([np.cos(angle), np.sin(angle)]).astype(np.float32)
    polar = np.stack([st, ct])[:, :, None].astype(np.float32)
    azim = np.stack([cp, sp]).astype(np.float32)
    series = series_table(n_box // 2)
    vmem = pl.BlockSpec(memory_space=pltpu.VMEM)
    smem = pl.BlockSpec(memory_space=pltpu.SMEM)
    chunk = (2, slab, 4 * lp)
    f32 = jnp.float32
    result = pl.pallas_call(
        functools.partial(kernel, (n_box, n_dir, count, lt, lp, slab)),
        out_shape=jax.ShapeDtypeStruct((n_dir, count) + chunk, f32),
        in_specs=[vmem, smem, smem, smem] + [vmem] * 8,
        out_specs=vmem,
        scratch_shapes=[
            pltpu.VMEM((count, 4, lt, lp), f32),
            pltpu.VMEM((count, 4, lt, lp), f32),
            pltpu.VMEM((4 * lt, 3 * lp), bf16),
            pltpu.VMEM((3 * lt, 8 * lp), bf16),
            pltpu.VMEM((2, 2 * lt, 2 * lp), f32),
            pltpu.VMEM((6 * lt, 8 * lp), bf16),
            pltpu.VMEM((8 * lt, 6 * lp), bf16),
            pltpu.VMEM((count, n_dir) + chunk, f32),
            pltpu.VMEM((n_dir, count) + chunk, f32),
            pltpu.VMEM((2, n_dir, count) + chunk, f32),
            pltpu.VMEM((2,) + chunk, f32),
            pltpu.SemaphoreType.DMA((count,)),
            pltpu.SemaphoreType.DMA((count,)),
            pltpu.SemaphoreType.DMA((count, n_dir)),
            pltpu.SemaphoreType.DMA((count, n_dir)),
            pltpu.SemaphoreType.DMA((2, count, n_dir)),
            pltpu.SemaphoreType.DMA((2, count, n_dir)),
        ],
        compiler_params=pltpu.CompilerParams(
            collective_id=0, has_side_effects=True, vmem_limit_bytes=48 << 20
        ),
    )(
        leaf_patterns, occupancy, pair_lists, jnp.asarray(series), jnp.asarray(c1),
        jnp.asarray(r1), jnp.asarray(r2), jnp.asarray(c2), jnp.asarray(ph1),
        jnp.asarray(ph2), jnp.asarray(polar), jnp.asarray(azim),
    )
    return result.reshape(1, 1, n_dir * count, *chunk)


def solution(mesh):
    placed = (P("box", "dir", None, None, None), P("box"), P())
    return jax.shard_map(
        functools.partial(per_device, mesh.shape["box"], mesh.shape["dir"]),
        mesh=mesh,
        in_specs=placed,
        out_specs=P("box", None, None, None, "dir", None),
        check_vma=False,
    )
```

```python
import functools

import jax
import jax.numpy as jnp
import numpy as np
from jax import lax
from jax.experimental import pallas as pl
from jax.experimental.pallas import tpu as pltpu
from jax.sharding import PartitionSpec as P

MESH = pl.DeviceIdType.MESH
LTR = 16
full_count = 16.0
phase_first = 16.0
phase_second = 64.0
translate_wave = 20.0


def interp_table(points, offset):
    orders = np.arange(points // 2 + 1, dtype=np.float64)
    weights = np.where((orders == 0) | (orders == points // 2), 1.0, 2.0) / points
    source = (np.arange(points) + offset) / points
    target = (np.arange(2 * points) + offset) / (2 * points)
    angle = 2.0 * np.pi * (target[:, None, None] - source[None, :, None]) * orders
    return (np.cos(angle) * weights).sum(-1)


def halves(table):
    high = np.asarray(table, np.float32).astype(jnp.bfloat16)
    low = (np.asarray(table, np.float64) - high.astype(np.float64)).astype(jnp.bfloat16)
    return high, low


def sines(rows, columns):
    theta = np.pi * (np.arange(rows) + 0.5) / rows
    phi = 2.0 * np.pi * np.arange(columns) / columns
    return np.sin(theta), np.cos(theta), np.cos(phi), np.sin(phi)


def center(g):
    return np.array([g % 4, g // 4 % 4, g // 16], np.float64)


def series_table(pairs):
    table = np.zeros((pairs, 2 * (3 + 2 * (LTR + 1))), np.float64)
    width = 3 + 2 * (LTR + 1)
    for g in range(pairs):
        for side, s in enumerate((g - 1, g + 1)):
            if not 0 <= s < pairs:
                continue
            r = center(g) - center(s)
            distance = np.sqrt((r * r).sum())
            x = translate_wave * distance
            now = (np.sin(x) - 1j * np.cos(x)) / x
            nxt = ((np.sin(x) - x * np.cos(x)) - 1j * (x * np.sin(x) + np.cos(x))) / x**2
            table[g, side * width : side * width + 3] = r / distance
            for degree in range(LTR + 1):
                value = (1j**degree) * (2 * degree + 1) * now
                table[g, side * width + 3 + 2 * degree] = value.real
                table[g, side * width + 4 + 2 * degree] = value.imag
                now, nxt = nxt, (2 * degree + 3) / x * nxt - now
    return table.astype(np.float32)


def split(value):
    high = value.astype(jnp.bfloat16)
    low = (value - high.astype(jnp.float32)).astype(jnp.bfloat16)
    return high, low


def dot(a, b):
    return jnp.dot(a, b, preferred_element_type=jnp.float32)


def kernel(
    sizes,
    leaf_in, occ_in, lists_in, series_in, c1_in, r1_in, r2_in, c2_in, ph1_in, ph2_in,
    polar_in, azim_in,
    out,
    leaf, occ, lists, series, c1, r1, r2, c2, ph1, ph2, polar, azim,
    mine, taken, lhs1, rhs1, first, rhs2, lhs2, ready, oper,
    loads, ls, lr, ds, dr,
):
    n_box, n_dir, count, lt, lp, slab = sizes
    box = lax.axis_index("box")
    me = lax.axis_index("dir")
    half = box % 2
    pair = box // 2
    has_lower = pair > 0
    has_upper = pair < n_box // 2 - 1
    partner = box + 1 - 2 * half
    row_start = pl.multiple_of(half * 2 * lt, 2 * lt)

    barrier = pltpu.get_barrier_semaphore()
    for o in range(1, n_dir):
        pl.semaphore_signal(
            barrier, inc=1, device_id=(box, (me + o) % n_dir), device_id_type=MESH
        )
    for present, by in ((has_lower, -2), (has_upper, 2)):
        @pl.when(present)
        def _():
            for start in (box, partner):
                pl.semaphore_signal(
                    barrier, inc=1, device_id=(start + by, me), device_id_type=MESH
                )

    half_rows = pl.ds(row_start, 2 * lt)
    pairs_in = (
        (leaf_in, leaf), (occ_in, occ), (lists_in, lists), (series_in, series),
        (polar_in.at[:, half_rows], polar), (azim_in, azim), (c1_in, c1), (r1_in, r1),
        (ph1_in, ph1), (r2_in.at[half], r2), (c2_in, c2), (ph2_in.at[:, half_rows], ph2),
    )
    copies = [
        pltpu.make_async_copy(source, target, loads.at[i])
        for i, (source, target) in enumerate(pairs_in)
    ]
    for copy in copies:
        copy.start()
    copies[1].wait()
    copies[0].wait()

    w0 = occ[0].astype(jnp.float32) / full_count
    w1 = occ[1].astype(jnp.float32) / full_count
    for r in range(count):
        for c in range(2):
            a = leaf[0, r, c] * w0
            b = leaf[1, r, c] * w1
            mine[r, c] = a + b
            mine[r, 2 + c] = b - a

    pl.semaphore_wait(
        barrier,
        n_dir - 1 + 2 * has_lower.astype(jnp.int32) + 2 * has_upper.astype(jnp.int32),
    )

    def l_copy(r, side, place):
        target = (box if place == 0 else partner) + 2 - 4 * side
        return pltpu.make_async_remote_copy(
            mine.at[r], taken.at[side, r, place], ls.at[side, r, place],
            lr.at[side, r, place], (target, me), device_id_type=MESH,
        )

    for r in range(count):
        for place in range(2):
            @pl.when(has_upper)
            def _():
                l_copy(r, 0, place).start()

            @pl.when(has_lower)
            def _():
                l_copy(r, 1, place).start()

    def d_copy(r, o):
        peer = (me + o) % n_dir
        return pltpu.make_async_remote_copy(
            ready.at[r, peer], out.at[me, r], ds.at[r, o], dr.at[r, n_dir - o],
            (box, peer), device_id_type=MESH,
        )

    def d_arrival(r, o):
        peer = (me + o) % n_dir
        return pltpu.make_async_remote_copy(
            ready.at[r, me], out.at[peer, r], ds.at[r, o], dr.at[r, o],
            (box, peer), device_id_type=MESH,
        )

    ready[...] = jnp.zeros(ready.shape, jnp.float32)
    for copy in copies[2:6]:
        copy.wait()

    slots = lists.shape[1]
    entries = lists.shape[2]
    width = 3 + 2 * (LTR + 1)
    for side in range(2):
        named = jnp.float32(0.0)
        for k in range(entries):
            chosen = lists[pair, 0, k]
            hit = chosen < slots if side == 0 else chosen >= 2 * slots
            named = named + jnp.where(hit, 1.0, 0.0)
        scale = named / entries
        base = side * width

        def oper_step(i, carry):
            rows = pl.ds(pl.multiple_of(i * 8, 8), 8)
            along_x = polar[0, rows] * azim[0:1]
            along_y = polar[0, rows] * azim[1:2]
            along_z = polar[1, rows] * jnp.ones_like(along_x)
            u = (
                series[pair, base] * along_x
                + series[pair, base + 1] * along_y
                + series[pair, base + 2] * along_z
            )
            now, nxt = jnp.ones_like(u), u
            real, imag = jnp.zeros_like(u), jnp.zeros_like(u)
            for degree in range(LTR + 1):
                real = real + series[pair, base + 3 + 2 * degree] * now
                imag = imag + series[pair, base + 4 + 2 * degree] * now
                now, nxt = nxt, (
                    ((2.0 * degree + 3.0) / (degree + 2.0)) * (u * nxt)
                    - ((degree + 1.0) / (degree + 2.0)) * now
                )
            oper[side, 0, rows] = real * scale
            oper[side, 1, rows] = imag * scale
            return carry

        lax.fori_loop(0, 2 * lt // 8, oper_step, 0)

    for copy in copies[6:]:
        copy.wait()

    def first_level(source):
        for k in range(4):
            high, low = split(source[k])
            rows = pl.ds(k * lt, lt)
            lhs1[rows, 0:lp] = high
            lhs1[rows, lp : 2 * lp] = low
            lhs1[rows, 2 * lp : 3 * lp] = high
        wide = dot(lhs1[...], c1[...])
        for k in range(4):
            high, low = split(wide[k * lt : (k + 1) * lt])
            columns = pl.ds(k * 2 * lp, 2 * lp)
            rhs1[0:lt, columns] = high
            rhs1[lt : 2 * lt, columns] = low
            rhs1[2 * lt : 3 * lt, columns] = high
        sr, si, dre, dim = [
            dot(r1[...], rhs1[:, k * 2 * lp : (k + 1) * 2 * lp]) for k in range(4)
        ]
        cosine, sine = ph1[0], ph1[1]
        return cosine * sr - sine * dim, cosine * si + sine * dre

    sign = (2 * half - 1).astype(jnp.float32)

    def add_side(r, side):
        for place in range(2):
            l_copy(r, side, place).wait_recv()
            fr, fi = first_level(taken.at[side, r, place])
            if place == 0:
                first[0] = fr
                first[1] = fi
        for k, value in enumerate(
            (first[0] + fr, first[1] + fi, (first[0] - fr) * sign, (first[1] - fi) * sign)
        ):
            high, low = split(value)
            columns = pl.ds(k * 2 * lp, 2 * lp)
            rhs2[0 : 2 * lt, columns] = high
            rhs2[2 * lt : 4 * lt, columns] = low
            rhs2[4 * lt : 6 * lt, columns] = high
        for k in range(4):
            high, low = split(dot(r2[...], rhs2[:, k * 2 * lp : (k + 1) * 2 * lp]))
            rows = pl.ds(k * 2 * lt, 2 * lt)
            lhs2[rows, 0 : 2 * lp] = high
            lhs2[rows, 2 * lp : 4 * lp] = low
            lhs2[rows, 4 * lp : 6 * lp] = high
        for d in range(n_dir):
            sr, si, dre, dim = [
                dot(lhs2[pl.ds(k * 2 * lt + d * slab, slab), :], c2[...]) for k in range(4)
            ]
            rows = pl.ds(d * slab, slab)
            cosine, sine = ph2[0, rows], ph2[1, rows]
            gr = cosine * sr - sine * dim
            gi = cosine * si + sine * dre
            pr, pi = oper[side, 0, rows], oper[side, 1, rows]
            ready[r, d, 0] += pr * gr - pi * gi
            ready[r, d, 1] += pr * gi + pi * gr

    def level_step(q, carry):
        r = q // 2
        side = q % 2

        @pl.when(jnp.where(side == 0, has_lower, has_upper))
        def _():
            add_side(r, side)

        @pl.when(side == 1)
        def _():
            for o in range(1, n_dir):
                d_copy(r, o).start()
            out[me, r] = ready[r, me]

        return carry

    lax.fori_loop(0, 2 * count, level_step, 0)

    for r in range(count):
        for o in range(1, n_dir):
            d_arrival(r, o).wait_recv()
            d_copy(r, o).wait_send()
        for place in range(2):
            @pl.when(has_upper)
            def _():
                l_copy(r, 0, place).wait_send()

            @pl.when(has_lower)
            def _():
                l_copy(r, 1, place).wait_send()


def per_device(n_box, n_dir, leaf_patterns, occupancy, pair_lists):
    _, count, _, lt, lp = leaf_patterns.shape
    assert leaf_patterns.shape[0] == 2
    slab = 2 * lt // n_dir
    bf16 = jnp.bfloat16
    first_high, first_low = halves(interp_table(lp, 0.0).T)
    c1 = np.concatenate([first_high, first_high, first_low], axis=0)
    row_high, row_low = halves(interp_table(lt, 0.5))
    r1 = np.concatenate([row_high, row_high, row_low], axis=1)
    row_high, row_low = halves(interp_table(2 * lt, 0.5).reshape(2, 2 * lt, 2 * lt))
    r2 = np.concatenate([row_high, row_high, row_low], axis=2)
    high, low = halves(interp_table(2 * lp, 0.0).T)
    c2 = np.concatenate([high, high, low], axis=0)
    st, _, cp, _ = sines(2 * lt, 2 * lp)
    angle = phase_first * st[:, None] * cp[None]
    ph1 = np.stack([np.cos(angle), np.sin(angle)]).astype(np.float32)
    st, ct, cp, sp = sines(4 * lt, 4 * lp)
    angle = phase_second * st[:, None] * sp[None]
    ph2 = np.stack([np.cos(angle), np.sin(angle)]).astype(np.float32)
    polar = np.stack([st, ct])[:, :, None].astype(np.float32)
    azim = np.stack([cp, sp]).astype(np.float32)
    series = series_table(n_box // 2)
    operands = (
        leaf_patterns, occupancy, pair_lists, series, c1, r1, r2, c2, ph1, ph2, polar, azim
    )
    chunk = (2, slab, 4 * lp)
    f32 = jnp.float32
    rows = 2 * lt
    result = pl.pallas_call(
        functools.partial(kernel, (n_box, n_dir, count, lt, lp, slab)),
        out_shape=jax.ShapeDtypeStruct((n_dir, count) + chunk, f32),
        in_specs=[pl.BlockSpec(memory_space=pltpu.HBM)] * len(operands),
        out_specs=pl.BlockSpec(memory_space=pltpu.VMEM),
        scratch_shapes=[
            pltpu.VMEM(leaf_patterns.shape, f32),
            pltpu.SMEM(occupancy.shape, jnp.int32),
            pltpu.SMEM(pair_lists.shape, jnp.int32),
            pltpu.SMEM(series.shape, f32),
            pltpu.VMEM(c1.shape, bf16),
            pltpu.VMEM(r1.shape, bf16),
            pltpu.VMEM(r2.shape[1:], bf16),
            pltpu.VMEM(c2.shape, bf16),
            pltpu.VMEM(ph1.shape, f32),
            pltpu.VMEM((2, rows, 4 * lp), f32),
            pltpu.VMEM((2, rows, 1), f32),
            pltpu.VMEM(azim.shape, f32),
            pltpu.VMEM((count, 4, lt, lp), f32),
            pltpu.VMEM((2, count, 2, 4, lt, lp), f32),
            pltpu.VMEM((4 * lt, 3 * lp), bf16),
            pltpu.VMEM((3 * lt, 8 * lp), bf16),
            pltpu.VMEM((2, rows, 2 * lp), f32),
            pltpu.VMEM((6 * lt, 8 * lp), bf16),
            pltpu.VMEM((8 * lt, 6 * lp), bf16),
            pltpu.VMEM((count, n_dir) + chunk, f32),
            pltpu.VMEM((2, 2, rows, 4 * lp), f32),
            pltpu.SemaphoreType.DMA((len(operands),)),
            pltpu.SemaphoreType.DMA((2, count, 2)),
            pltpu.SemaphoreType.DMA((2, count, 2)),
            pltpu.SemaphoreType.DMA((count, n_dir)),
            pltpu.SemaphoreType.DMA((count, n_dir)),
        ],
        compiler_params=pltpu.CompilerParams(
            collective_id=0, has_side_effects=True, vmem_limit_bytes=64500000
        ),
    )(*[jnp.asarray(operand) for operand in operands])
    return result.reshape(1, 1, n_dir * count, *chunk)


def solution(mesh):
    placed = (P("box", "dir", None, None, None), P("box"), P())
    return jax.shard_map(
        functools.partial(per_device, mesh.shape["box"], mesh.shape["dir"]),
        mesh=mesh,
        in_specs=placed,
        out_specs=P("box", None, None, None, "dir", None),
        check_vma=False,
    )
```

```python
import functools

import jax
import jax.numpy as jnp
import numpy as np
from jax import lax
from jax.experimental import pallas as pl
from jax.experimental.pallas import tpu as pltpu
from jax.sharding import PartitionSpec as P

MESH = pl.DeviceIdType.MESH
LTR = 16
full_count = 16.0
phase_first = 16.0
phase_second = 64.0
translate_wave = 20.0


def interp_table(points, offset):
    orders = np.arange(points // 2 + 1, dtype=np.float64)
    weights = np.where((orders == 0) | (orders == points // 2), 1.0, 2.0) / points
    source = (np.arange(points) + offset) / points
    target = (np.arange(2 * points) + offset) / (2 * points)
    angle = 2.0 * np.pi * (target[:, None, None] - source[None, :, None]) * orders
    return (np.cos(angle) * weights).sum(-1)


def halves(table):
    high = np.asarray(table, np.float32).astype(jnp.bfloat16)
    low = (np.asarray(table, np.float64) - high.astype(np.float64)).astype(jnp.bfloat16)
    return high, low


def sines(rows, columns):
    theta = np.pi * (np.arange(rows) + 0.5) / rows
    phi = 2.0 * np.pi * np.arange(columns) / columns
    return np.sin(theta), np.cos(theta), np.cos(phi), np.sin(phi)


def center(g):
    return np.array([g % 4, g // 4 % 4, g // 16], np.float64)


def series_table(pairs):
    table = np.zeros((pairs, 2 * (3 + 2 * (LTR + 1))), np.float64)
    width = 3 + 2 * (LTR + 1)
    for g in range(pairs):
        for side, s in enumerate((g - 1, g + 1)):
            if not 0 <= s < pairs:
                continue
            r = center(g) - center(s)
            distance = np.sqrt((r * r).sum())
            x = translate_wave * distance
            now = (np.sin(x) - 1j * np.cos(x)) / x
            nxt = ((np.sin(x) - x * np.cos(x)) - 1j * (x * np.sin(x) + np.cos(x))) / x**2
            table[g, side * width : side * width + 3] = r / distance
            for degree in range(LTR + 1):
                value = (1j**degree) * (2 * degree + 1) * now
                table[g, side * width + 3 + 2 * degree] = value.real
                table[g, side * width + 4 + 2 * degree] = value.imag
                now, nxt = nxt, (2 * degree + 3) / x * nxt - now
    return table.astype(np.float32)


def split(value):
    high = value.astype(jnp.bfloat16)
    low = (value - high.astype(jnp.float32)).astype(jnp.bfloat16)
    return high, low


def dot(a, b):
    return jnp.dot(a, b, preferred_element_type=jnp.float32)


def kernel(
    sizes,
    leaf_in, occ_in, lists_in, series_in, c1_in, r1_in, r2_in, c2_in, ph1_in, ph2_in,
    polar_in, azim_in,
    out,
    leaf, occ, lists, series, c1, r1, r2, c2, ph1, ph2, polar, azim,
    mine, taken, lhs1, rhs1, first, rhs2, lhs2, wide, ready, oper,
    loads, ls, lr, ds, dr,
):
    n_box, n_dir, count, lt, lp, slab = sizes
    box = lax.axis_index("box")
    me = lax.axis_index("dir")
    half = box % 2
    pair = box // 2
    has_lower = pair > 0
    has_upper = pair < n_box // 2 - 1
    partner = box + 1 - 2 * half
    row_start = pl.multiple_of(half * 2 * lt, 2 * lt)

    barrier = pltpu.get_barrier_semaphore()
    for o in range(1, n_dir):
        pl.semaphore_signal(
            barrier, inc=1, device_id=(box, (me + o) % n_dir), device_id_type=MESH
        )
    for present, by in ((has_lower, -2), (has_upper, 2)):
        @pl.when(present)
        def _():
            for start in (box, partner):
                pl.semaphore_signal(
                    barrier, inc=1, device_id=(start + by, me), device_id_type=MESH
                )

    half_rows = pl.ds(row_start, 2 * lt)
    pairs_in = (
        (leaf_in, leaf), (occ_in, occ), (lists_in, lists), (series_in, series),
        (polar_in.at[:, half_rows], polar), (azim_in, azim), (c1_in, c1), (r1_in, r1),
        (ph1_in, ph1), (r2_in.at[half], r2), (c2_in, c2), (ph2_in.at[:, half_rows], ph2),
    )
    copies = [
        pltpu.make_async_copy(source, target, loads.at[i])
        for i, (source, target) in enumerate(pairs_in)
    ]
    for copy in copies:
        copy.start()
    copies[1].wait()
    copies[0].wait()

    w0 = occ[0].astype(jnp.float32) / full_count
    w1 = occ[1].astype(jnp.float32) / full_count
    for r in range(count):
        for c in range(2):
            a = leaf[0, r, c] * w0
            b = leaf[1, r, c] * w1
            mine[r, c] = a + b
            mine[r, 2 + c] = b - a

    pl.semaphore_wait(
        barrier,
        n_dir - 1 + 2 * has_lower.astype(jnp.int32) + 2 * has_upper.astype(jnp.int32),
    )

    def l_copy(r, side, place):
        target = (box if place == 0 else partner) + 2 - 4 * side
        return pltpu.make_async_remote_copy(
            mine.at[r], taken.at[side, r, place], ls.at[side, r, place],
            lr.at[side, r, place], (target, me), device_id_type=MESH,
        )

    for r in range(count):
        for place in range(2):
            @pl.when(has_upper)
            def _():
                l_copy(r, 0, place).start()

            @pl.when(has_lower)
            def _():
                l_copy(r, 1, place).start()

    def d_copy(r, o):
        peer = (me + o) % n_dir
        return pltpu.make_async_remote_copy(
            ready.at[r, peer], out.at[me, r], ds.at[r, o], dr.at[r, n_dir - o],
            (box, peer), device_id_type=MESH,
        )

    def d_arrival(r, o):
        peer = (me + o) % n_dir
        return pltpu.make_async_remote_copy(
            ready.at[r, me], out.at[peer, r], ds.at[r, o], dr.at[r, o],
            (box, peer), device_id_type=MESH,
        )

    ready[...] = jnp.zeros(ready.shape, jnp.float32)
    for copy in copies[2:6]:
        copy.wait()

    slots = lists.shape[1]
    entries = lists.shape[2]
    width = 3 + 2 * (LTR + 1)
    for side in range(2):
        named = jnp.float32(0.0)
        for k in range(entries):
            chosen = lists[pair, 0, k]
            hit = chosen < slots if side == 0 else chosen >= 2 * slots
            named = named + jnp.where(hit, 1.0, 0.0)
        scale = named / entries
        base = side * width

        def oper_step(i, carry):
            rows = pl.ds(pl.multiple_of(i * 8, 8), 8)
            along_x = polar[0, rows] * azim[0:1]
            along_y = polar[0, rows] * azim[1:2]
            along_z = polar[1, rows] * jnp.ones_like(along_x)
            u = (
                series[pair, base] * along_x
                + series[pair, base + 1] * along_y
                + series[pair, base + 2] * along_z
            )
            now, nxt = jnp.ones_like(u), u
            real, imag = jnp.zeros_like(u), jnp.zeros_like(u)
            for degree in range(LTR + 1):
                real = real + series[pair, base + 3 + 2 * degree] * now
                imag = imag + series[pair, base + 4 + 2 * degree] * now
                now, nxt = nxt, (
                    ((2.0 * degree + 3.0) / (degree + 2.0)) * (u * nxt)
                    - ((degree + 1.0) / (degree + 2.0)) * now
                )
            oper[side, 0, rows] = real * scale
            oper[side, 1, rows] = imag * scale
            return carry

        lax.fori_loop(0, 2 * lt // 8, oper_step, 0)

    for copy in copies[6:]:
        copy.wait()

    def first_level(source):
        for k in range(4):
            high, low = split(source[k])
            rows = pl.ds(k * lt, lt)
            lhs1[rows, 0:lp] = high
            lhs1[rows, lp : 2 * lp] = low
            lhs1[rows, 2 * lp : 3 * lp] = high
        stretched = dot(lhs1[...], c1[...])
        for k in range(4):
            high, low = split(stretched[k * lt : (k + 1) * lt])
            columns = pl.ds(k * 2 * lp, 2 * lp)
            rhs1[0:lt, columns] = high
            rhs1[lt : 2 * lt, columns] = low
            rhs1[2 * lt : 3 * lt, columns] = high
        sr, si, dre, dim = [
            dot(r1[...], rhs1[:, k * 2 * lp : (k + 1) * 2 * lp]) for k in range(4)
        ]
        cosine, sine = ph1[0], ph1[1]
        return cosine * sr - sine * dim, cosine * si + sine * dre

    sign = (2 * half - 1).astype(jnp.float32)

    def add_side(r, side):
        for place in range(2):
            l_copy(r, side, place).wait_recv()
            fr, fi = first_level(taken.at[side, r, place])
            if place == 0:
                first[0] = fr
                first[1] = fi
        for k, value in enumerate(
            (first[0] + fr, first[1] + fi, (first[0] - fr) * sign, (first[1] - fi) * sign)
        ):
            high, low = split(value)
            columns = pl.ds(k * 2 * lp, 2 * lp)
            rhs2[0 : 2 * lt, columns] = high
            rhs2[2 * lt : 4 * lt, columns] = low
            rhs2[4 * lt : 6 * lt, columns] = high
        for k in range(4):
            high, low = split(dot(r2[...], rhs2[:, k * 2 * lp : (k + 1) * 2 * lp]))
            rows = pl.ds(k * 2 * lt, 2 * lt)
            lhs2[rows, 0 : 2 * lp] = high
            lhs2[rows, 2 * lp : 4 * lp] = low
            lhs2[rows, 4 * lp : 6 * lp] = high
        wide[...] = dot(lhs2[...], c2[...])
        for d in range(n_dir):
            sr, si, dre, dim = [wide[pl.ds(k * 2 * lt + d * slab, slab), :] for k in range(4)]
            rows = pl.ds(d * slab, slab)
            cosine, sine = ph2[0, rows], ph2[1, rows]
            gr = cosine * sr - sine * dim
            gi = cosine * si + sine * dre
            pr, pi = oper[side, 0, rows], oper[side, 1, rows]
            ready[r, d, 0] += pr * gr - pi * gi
            ready[r, d, 1] += pr * gi + pi * gr

    def level_step(q, carry):
        r = q // 2
        side = q % 2

        @pl.when(jnp.where(side == 0, has_lower, has_upper))
        def _():
            add_side(r, side)

        @pl.when(side == 1)
        def _():
            for o in range(1, n_dir):
                d_copy(r, o).start()
            out[me, r] = ready[r, me]

        return carry

    lax.fori_loop(0, 2 * count, level_step, 0)

    for r in range(count):
        for o in range(1, n_dir):
            d_arrival(r, o).wait_recv()
            d_copy(r, o).wait_send()
        for place in range(2):
            @pl.when(has_upper)
            def _():
                l_copy(r, 0, place).wait_send()

            @pl.when(has_lower)
            def _():
                l_copy(r, 1, place).wait_send()


def per_device(n_box, n_dir, leaf_patterns, occupancy, pair_lists):
    _, count, _, lt, lp = leaf_patterns.shape
    assert leaf_patterns.shape[0] == 2
    slab = 2 * lt // n_dir
    bf16 = jnp.bfloat16
    first_high, first_low = halves(interp_table(lp, 0.0).T)
    c1 = np.concatenate([first_high, first_high, first_low], axis=0)
    row_high, row_low = halves(interp_table(lt, 0.5))
    r1 = np.concatenate([row_high, row_high, row_low], axis=1)
    row_high, row_low = halves(interp_table(2 * lt, 0.5).reshape(2, 2 * lt, 2 * lt))
    r2 = np.concatenate([row_high, row_high, row_low], axis=2)
    high, low = halves(interp_table(2 * lp, 0.0).T)
    c2 = np.concatenate([high, high, low], axis=0)
    st, _, cp, _ = sines(2 * lt, 2 * lp)
    angle = phase_first * st[:, None] * cp[None]
    ph1 = np.stack([np.cos(angle), np.sin(angle)]).astype(np.float32)
    st, ct, cp, sp = sines(4 * lt, 4 * lp)
    angle = phase_second * st[:, None] * sp[None]
    ph2 = np.stack([np.cos(angle), np.sin(angle)]).astype(np.float32)
    polar = np.stack([st, ct])[:, :, None].astype(np.float32)
    azim = np.stack([cp, sp]).astype(np.float32)
    series = series_table(n_box // 2)
    operands = (
        leaf_patterns, occupancy, pair_lists, series, c1, r1, r2, c2, ph1, ph2, polar, azim
    )
    chunk = (2, slab, 4 * lp)
    f32 = jnp.float32
    rows = 2 * lt
    result = pl.pallas_call(
        functools.partial(kernel, (n_box, n_dir, count, lt, lp, slab)),
        out_shape=jax.ShapeDtypeStruct((n_dir, count) + chunk, f32),
        in_specs=[pl.BlockSpec(memory_space=pltpu.HBM)] * len(operands),
        out_specs=pl.BlockSpec(memory_space=pltpu.VMEM),
        scratch_shapes=[
            pltpu.VMEM(leaf_patterns.shape, f32),
            pltpu.SMEM(occupancy.shape, jnp.int32),
            pltpu.SMEM(pair_lists.shape, jnp.int32),
            pltpu.SMEM(series.shape, f32),
            pltpu.VMEM(c1.shape, bf16),
            pltpu.VMEM(r1.shape, bf16),
            pltpu.VMEM(r2.shape[1:], bf16),
            pltpu.VMEM(c2.shape, bf16),
            pltpu.VMEM(ph1.shape, f32),
            pltpu.VMEM((2, rows, 4 * lp), f32),
            pltpu.VMEM((2, rows, 1), f32),
            pltpu.VMEM(azim.shape, f32),
            pltpu.VMEM((count, 4, lt, lp), f32),
            pltpu.VMEM((2, count, 2, 4, lt, lp), f32),
            pltpu.VMEM((4 * lt, 3 * lp), bf16),
            pltpu.VMEM((3 * lt, 8 * lp), bf16),
            pltpu.VMEM((2, rows, 2 * lp), f32),
            pltpu.VMEM((6 * lt, 8 * lp), bf16),
            pltpu.VMEM((8 * lt, 6 * lp), bf16),
            pltpu.VMEM((8 * lt, 4 * lp), f32),
            pltpu.VMEM((count, n_dir) + chunk, f32),
            pltpu.VMEM((2, 2, rows, 4 * lp), f32),
            pltpu.SemaphoreType.DMA((len(operands),)),
            pltpu.SemaphoreType.DMA((2, count, 2)),
            pltpu.SemaphoreType.DMA((2, count, 2)),
            pltpu.SemaphoreType.DMA((count, n_dir)),
            pltpu.SemaphoreType.DMA((count, n_dir)),
        ],
        compiler_params=pltpu.CompilerParams(
            collective_id=0, has_side_effects=True, vmem_limit_bytes=64500000
        ),
    )(*[jnp.asarray(operand) for operand in operands])
    return result.reshape(1, 1, n_dir * count, *chunk)


def solution(mesh):
    placed = (P("box", "dir", None, None, None), P("box"), P())
    return jax.shard_map(
        functools.partial(per_device, mesh.shape["box"], mesh.shape["dir"]),
        mesh=mesh,
        in_specs=placed,
        out_specs=P("box", None, None, None, "dir", None),
        check_vma=False,
    )
```

```python
import functools

import jax
import jax.numpy as jnp
import numpy as np
from jax import lax
from jax.experimental import pallas as pl
from jax.experimental.pallas import tpu as pltpu
from jax.sharding import PartitionSpec as P

MESH = pl.DeviceIdType.MESH
LTR = 16
full_count = 16.0
phase_first = 16.0
phase_second = 64.0
translate_wave = 20.0


def interp_table(points, offset):
    orders = np.arange(points // 2 + 1, dtype=np.float64)
    weights = np.where((orders == 0) | (orders == points // 2), 1.0, 2.0) / points
    source = (np.arange(points) + offset) / points
    target = (np.arange(2 * points) + offset) / (2 * points)
    angle = 2.0 * np.pi * (target[:, None, None] - source[None, :, None]) * orders
    return (np.cos(angle) * weights).sum(-1)


def halves(table):
    high = np.asarray(table, np.float32).astype(jnp.bfloat16)
    low = (np.asarray(table, np.float64) - high.astype(np.float64)).astype(jnp.bfloat16)
    return high, low


def sines(rows, columns):
    theta = np.pi * (np.arange(rows) + 0.5) / rows
    phi = 2.0 * np.pi * np.arange(columns) / columns
    return np.sin(theta), np.cos(theta), np.cos(phi), np.sin(phi)


def center(g):
    return np.array([g % 4, g // 4 % 4, g // 16], np.float64)


def series_table(pairs):
    table = np.zeros((pairs, 2 * (3 + 2 * (LTR + 1))), np.float64)
    width = 3 + 2 * (LTR + 1)
    for g in range(pairs):
        for side, s in enumerate((g - 1, g + 1)):
            if not 0 <= s < pairs:
                continue
            r = center(g) - center(s)
            distance = np.sqrt((r * r).sum())
            x = translate_wave * distance
            now = (np.sin(x) - 1j * np.cos(x)) / x
            nxt = ((np.sin(x) - x * np.cos(x)) - 1j * (x * np.sin(x) + np.cos(x))) / x**2
            table[g, side * width : side * width + 3] = r / distance
            for degree in range(LTR + 1):
                value = (1j**degree) * (2 * degree + 1) * now
                table[g, side * width + 3 + 2 * degree] = value.real
                table[g, side * width + 4 + 2 * degree] = value.imag
                now, nxt = nxt, (2 * degree + 3) / x * nxt - now
    return table.astype(np.float32)


def split(value):
    high = value.astype(jnp.bfloat16)
    low = (value - high.astype(jnp.float32)).astype(jnp.bfloat16)
    return high, low


def dot(a, b):
    return jnp.dot(a, b, preferred_element_type=jnp.float32)


def kernel(
    sizes,
    leaf_in, occ_in, lists_in, series_in, c1_in, r1_in, r2_in, c2_in, ph1_in, ph2_in,
    polar_in, azim_in,
    out,
    leaf, occ, lists, series, c1, r1, r2, c2, ph1, ph2, polar, azim,
    mine, taken, lhs1, rhs1, first, rhs2, lhs2, wide, ready, oper,
    loads, ls, lr, ds, dr,
):
    n_box, n_dir, count, lt, lp, slab = sizes
    box = lax.axis_index("box")
    me = lax.axis_index("dir")
    half = box % 2
    pair = box // 2
    has_lower = pair > 0
    has_upper = pair < n_box // 2 - 1
    partner = box + 1 - 2 * half
    row_start = pl.multiple_of(half * 2 * lt, 2 * lt)

    barrier = pltpu.get_barrier_semaphore()
    for o in range(1, n_dir):
        pl.semaphore_signal(
            barrier, inc=1, device_id=(box, (me + o) % n_dir), device_id_type=MESH
        )
    for present, by in ((has_lower, -2), (has_upper, 2)):
        @pl.when(present)
        def _():
            for start in (box, partner):
                pl.semaphore_signal(
                    barrier, inc=1, device_id=(start + by, me), device_id_type=MESH
                )

    half_rows = pl.ds(row_start, 2 * lt)
    pairs_in = (
        (leaf_in, leaf), (occ_in, occ), (lists_in, lists), (series_in, series),
        (polar_in.at[:, half_rows], polar), (azim_in, azim), (c1_in, c1), (r1_in, r1),
        (ph1_in, ph1), (r2_in.at[half], r2), (c2_in, c2), (ph2_in.at[:, half_rows], ph2),
    )
    copies = [
        pltpu.make_async_copy(source, target, loads.at[i])
        for i, (source, target) in enumerate(pairs_in)
    ]
    for copy in copies:
        copy.start()
    copies[1].wait()
    copies[0].wait()

    w0 = occ[0].astype(jnp.float32) / full_count
    w1 = occ[1].astype(jnp.float32) / full_count
    for r in range(count):
        for c in range(2):
            a = leaf[0, r, c] * w0
            b = leaf[1, r, c] * w1
            mine[r, c] = a + b
            mine[r, 2 + c] = b - a

    pl.semaphore_wait(
        barrier,
        n_dir - 1 + 2 * has_lower.astype(jnp.int32) + 2 * has_upper.astype(jnp.int32),
    )

    def l_copy(r, side, place):
        target = (box if place == 0 else partner) + 2 - 4 * side
        return pltpu.make_async_remote_copy(
            mine.at[r], taken.at[side, r, place], ls.at[side, r, place],
            lr.at[side, r, place], (target, me), device_id_type=MESH,
        )

    for r in range(count):
        for place in range(2):
            @pl.when(has_upper)
            def _():
                l_copy(r, 0, place).start()

            @pl.when(has_lower)
            def _():
                l_copy(r, 1, place).start()

    def d_copy(r, o):
        peer = (me + o) % n_dir
        return pltpu.make_async_remote_copy(
            ready.at[r, peer], out.at[me, r], ds.at[r, o], dr.at[r, n_dir - o],
            (box, peer), device_id_type=MESH,
        )

    def d_arrival(r, o):
        peer = (me + o) % n_dir
        return pltpu.make_async_remote_copy(
            ready.at[r, me], out.at[peer, r], ds.at[r, o], dr.at[r, o],
            (box, peer), device_id_type=MESH,
        )

    ready[...] = jnp.zeros(ready.shape, jnp.float32)
    for copy in copies[2:6]:
        copy.wait()

    slots = lists.shape[1]
    entries = lists.shape[2]
    width = 3 + 2 * (LTR + 1)
    for side in range(2):
        named = jnp.float32(0.0)
        for k in range(entries):
            chosen = lists[pair, 0, k]
            hit = chosen < slots if side == 0 else chosen >= 2 * slots
            named = named + jnp.where(hit, 1.0, 0.0)
        scale = named / entries
        base = side * width

        def oper_step(i, carry):
            rows = pl.ds(pl.multiple_of(i * 8, 8), 8)
            along_x = polar[0, rows] * azim[0:1]
            along_y = polar[0, rows] * azim[1:2]
            along_z = polar[1, rows] * jnp.ones_like(along_x)
            u = (
                series[pair, base] * along_x
                + series[pair, base + 1] * along_y
                + series[pair, base + 2] * along_z
            )
            now, nxt = jnp.ones_like(u), u
            real, imag = jnp.zeros_like(u), jnp.zeros_like(u)
            for degree in range(LTR + 1):
                real = real + series[pair, base + 3 + 2 * degree] * now
                imag = imag + series[pair, base + 4 + 2 * degree] * now
                now, nxt = nxt, (
                    ((2.0 * degree + 3.0) / (degree + 2.0)) * (u * nxt)
                    - ((degree + 1.0) / (degree + 2.0)) * now
                )
            oper[side, 0, rows] = real * scale
            oper[side, 1, rows] = imag * scale
            return carry

        lax.fori_loop(0, 2 * lt // 8, oper_step, 0)

    for copy in copies[6:]:
        copy.wait()

    def first_level(source):
        for k in range(4):
            high, low = split(source[k])
            rows = pl.ds(k * lt, lt)
            lhs1[rows, 0:lp] = high
            lhs1[rows, lp : 2 * lp] = low
            lhs1[rows, 2 * lp : 3 * lp] = high
        stretched = dot(lhs1[...], c1[...])
        for k in range(4):
            high, low = split(stretched[k * lt : (k + 1) * lt])
            columns = pl.ds(k * 2 * lp, 2 * lp)
            rhs1[0:lt, columns] = high
            rhs1[lt : 2 * lt, columns] = low
            rhs1[2 * lt : 3 * lt, columns] = high
        sr, si, dre, dim = [
            dot(r1[...], rhs1[:, k * 2 * lp : (k + 1) * 2 * lp]) for k in range(4)
        ]
        cosine, sine = ph1[0], ph1[1]
        return cosine * sr - sine * dim, cosine * si + sine * dre

    sign = (2 * half - 1).astype(jnp.float32)

    def add_side(r, side):
        for place in range(2):
            l_copy(r, side, place).wait_recv()
            fr, fi = first_level(taken.at[side, r, place])
            if place == 0:
                first[0] = fr
                first[1] = fi
        for k, value in enumerate(
            (first[0] + fr, first[1] + fi, (first[0] - fr) * sign, (first[1] - fi) * sign)
        ):
            high, low = split(value)
            columns = pl.ds(k * 2 * lp, 2 * lp)
            rhs2[0 : 2 * lt, columns] = high
            rhs2[2 * lt : 4 * lt, columns] = low
            rhs2[4 * lt : 6 * lt, columns] = high
        for k in range(4):
            high, low = split(dot(r2[...], rhs2[:, k * 2 * lp : (k + 1) * 2 * lp]))
            rows = pl.ds(k * 2 * lt, 2 * lt)
            lhs2[rows, 0 : 2 * lp] = high
            lhs2[rows, 2 * lp : 4 * lp] = low
            lhs2[rows, 4 * lp : 6 * lp] = high
        wide[...] = dot(lhs2[...], c2[...])
        for d in range(n_dir):
            sr, si, dre, dim = [wide[pl.ds(k * 2 * lt + d * slab, slab), :] for k in range(4)]
            rows = pl.ds(d * slab, slab)
            cosine, sine = ph2[0, rows], ph2[1, rows]
            gr = cosine * sr - sine * dim
            gi = cosine * si + sine * dre
            pr, pi = oper[side, 0, rows], oper[side, 1, rows]
            ready[r, d, 0] += pr * gr - pi * gi
            ready[r, d, 1] += pr * gi + pi * gr

    def level_step(q, carry):
        r = q // 2
        side = q % 2

        @pl.when(jnp.where(side == 0, has_lower, has_upper))
        def _():
            add_side(r, side)

        @pl.when(side == 1)
        def _():
            for o in range(1, n_dir):
                d_copy(r, o).start()
            out[me, r] = ready[r, me]

        return carry

    lax.fori_loop(0, 2 * count, level_step, 0)

    for r in range(count):
        for o in range(1, n_dir):
            d_arrival(r, o).wait_recv()
            d_copy(r, o).wait_send()
        for place in range(2):
            @pl.when(has_upper)
            def _():
                l_copy(r, 0, place).wait_send()

            @pl.when(has_lower)
            def _():
                l_copy(r, 1, place).wait_send()


def per_device(n_box, n_dir, leaf_patterns, occupancy, pair_lists):
    _, count, _, lt, lp = leaf_patterns.shape
    assert leaf_patterns.shape[0] == 2
    slab = 2 * lt // n_dir
    bf16 = jnp.bfloat16
    first_high, first_low = halves(interp_table(lp, 0.0).T)
    c1 = np.concatenate([first_high, first_high, first_low], axis=0)
    row_high, row_low = halves(interp_table(lt, 0.5))
    r1 = np.concatenate([row_high, row_high, row_low], axis=1)
    row_high, row_low = halves(interp_table(2 * lt, 0.5).reshape(2, 2 * lt, 2 * lt))
    r2 = np.concatenate([row_high, row_high, row_low], axis=2)
    high, low = halves(interp_table(2 * lp, 0.0).T)
    c2 = np.concatenate([high, high, low], axis=0)
    st, _, cp, _ = sines(2 * lt, 2 * lp)
    angle = phase_first * st[:, None] * cp[None]
    ph1 = np.stack([np.cos(angle), np.sin(angle)]).astype(np.float32)
    st, ct, cp, sp = sines(4 * lt, 4 * lp)
    angle = phase_second * st[:, None] * sp[None]
    ph2 = np.stack([np.cos(angle), np.sin(angle)]).astype(np.float32)
    polar = np.stack([st, ct])[:, :, None].astype(np.float32)
    azim = np.stack([cp, sp]).astype(np.float32)
    series = series_table(n_box // 2)
    operands = (
        leaf_patterns, occupancy, pair_lists, series, c1, r1, r2, c2, ph1, ph2, polar, azim
    )
    chunk = (2, slab, 4 * lp)
    f32 = jnp.float32
    rows = 2 * lt
    result = pl.pallas_call(
        functools.partial(kernel, (n_box, n_dir, count, lt, lp, slab)),
        out_shape=jax.ShapeDtypeStruct((n_dir, count) + chunk, f32),
        in_specs=[pl.BlockSpec(memory_space=pltpu.HBM)] * len(operands),
        out_specs=pl.BlockSpec(memory_space=pltpu.VMEM),
        scratch_shapes=[
            pltpu.VMEM(leaf_patterns.shape, f32),
            pltpu.SMEM(occupancy.shape, jnp.int32),
            pltpu.SMEM(pair_lists.shape, jnp.int32),
            pltpu.SMEM(series.shape, f32),
            pltpu.VMEM(c1.shape, bf16),
            pltpu.VMEM(r1.shape, bf16),
            pltpu.VMEM(r2.shape[1:], bf16),
            pltpu.VMEM(c2.shape, bf16),
            pltpu.VMEM(ph1.shape, f32),
            pltpu.VMEM((2, rows, 4 * lp), f32),
            pltpu.VMEM((2, rows, 1), f32),
            pltpu.VMEM(azim.shape, f32),
            pltpu.VMEM((count, 4, lt, lp), f32),
            pltpu.VMEM((2, count, 2, 4, lt, lp), f32),
            pltpu.VMEM((4 * lt, 3 * lp), bf16),
            pltpu.VMEM((3 * lt, 8 * lp), bf16),
            pltpu.VMEM((2, rows, 2 * lp), f32),
            pltpu.VMEM((6 * lt, 8 * lp), bf16),
            pltpu.VMEM((8 * lt, 6 * lp), bf16),
            pltpu.VMEM((8 * lt, 4 * lp), f32),
            pltpu.VMEM((count, n_dir) + chunk, f32),
            pltpu.VMEM((2, 2, rows, 4 * lp), f32),
            pltpu.SemaphoreType.DMA((len(operands),)),
            pltpu.SemaphoreType.DMA((2, count, 2)),
            pltpu.SemaphoreType.DMA((2, count, 2)),
            pltpu.SemaphoreType.DMA((count, n_dir)),
            pltpu.SemaphoreType.DMA((count, n_dir)),
        ],
        compiler_params=pltpu.CompilerParams(
            collective_id=0, has_side_effects=True, vmem_limit_bytes=48 << 20
        ),
    )(*[pltpu.with_memory_space_constraint(jnp.asarray(operand), pltpu.HBM) for operand in operands])
    return result.reshape(1, 1, n_dir * count, *chunk)


def solution(mesh):
    placed = (P("box", "dir", None, None, None), P("box"), P())
    return jax.shard_map(
        functools.partial(per_device, mesh.shape["box"], mesh.shape["dir"]),
        mesh=mesh,
        in_specs=placed,
        out_specs=P("box", None, None, None, "dir", None),
        check_vma=False,
    )
```

```python
import functools

import jax
import jax.numpy as jnp
import numpy as np
from jax import lax
from jax.experimental import pallas as pl
from jax.experimental.pallas import tpu as pltpu
from jax.sharding import PartitionSpec as P

MESH = pl.DeviceIdType.MESH
LTR = 16
full_count = 16.0
phase_first = 16.0
phase_second = 64.0
translate_wave = 20.0


def interp_table(points, offset):
    orders = np.arange(points // 2 + 1, dtype=np.float64)
    weights = np.where((orders == 0) | (orders == points // 2), 1.0, 2.0) / points
    source = (np.arange(points) + offset) / points
    target = (np.arange(2 * points) + offset) / (2 * points)
    angle = 2.0 * np.pi * (target[:, None, None] - source[None, :, None]) * orders
    return (np.cos(angle) * weights).sum(-1)


def halves(table):
    high = np.asarray(table, np.float32).astype(jnp.bfloat16)
    low = (np.asarray(table, np.float64) - high.astype(np.float64)).astype(jnp.bfloat16)
    return high, low


def sines(rows, columns):
    theta = np.pi * (np.arange(rows) + 0.5) / rows
    phi = 2.0 * np.pi * np.arange(columns) / columns
    return np.sin(theta), np.cos(theta), np.cos(phi), np.sin(phi)


def center(g):
    return np.array([g % 4, g // 4 % 4, g // 16], np.float64)


def series_table(pairs):
    table = np.zeros((pairs, 2 * (3 + 2 * (LTR + 1))), np.float64)
    width = 3 + 2 * (LTR + 1)
    for g in range(pairs):
        for side, s in enumerate((g - 1, g + 1)):
            if not 0 <= s < pairs:
                continue
            r = center(g) - center(s)
            distance = np.sqrt((r * r).sum())
            x = translate_wave * distance
            now = (np.sin(x) - 1j * np.cos(x)) / x
            nxt = ((np.sin(x) - x * np.cos(x)) - 1j * (x * np.sin(x) + np.cos(x))) / x**2
            table[g, side * width : side * width + 3] = r / distance
            for degree in range(LTR + 1):
                value = (1j**degree) * (2 * degree + 1) * now
                table[g, side * width + 3 + 2 * degree] = value.real
                table[g, side * width + 4 + 2 * degree] = value.imag
                now, nxt = nxt, (2 * degree + 3) / x * nxt - now
    return table.astype(np.float32)


def split(value):
    high = value.astype(jnp.bfloat16)
    low = (value - high.astype(jnp.float32)).astype(jnp.bfloat16)
    return high, low


def dot(a, b):
    return jnp.dot(a, b, preferred_element_type=jnp.float32)


def kernel(
    sizes,
    leaf_in, occ_in, lists_in, series_in, c1_in, r1_in, r2_in, c2_in, ph1_in, ph2_in,
    polar_in, azim_in,
    out,
    leaf, occ, lists, series, c1, r1, r2, c2, ph1, ph2, polar, azim,
    mine, taken, lhs1, rhs1, first, rhs2, lhs2, wide, ready, oper,
    loads, ls, lr, ds, dr,
):
    n_box, n_dir, count, lt, lp, slab = sizes
    box = lax.axis_index("box")
    me = lax.axis_index("dir")
    half = box % 2
    pair = box // 2
    has_lower = pair > 0
    has_upper = pair < n_box // 2 - 1
    partner = box + 1 - 2 * half
    row_start = pl.multiple_of(half * 2 * lt, 2 * lt)

    barrier = pltpu.get_barrier_semaphore()
    for o in range(1, n_dir):
        pl.semaphore_signal(
            barrier, inc=1, device_id=(box, (me + o) % n_dir), device_id_type=MESH
        )
    for present, by in ((has_lower, -2), (has_upper, 2)):
        @pl.when(present)
        def _():
            for start in (box, partner):
                pl.semaphore_signal(
                    barrier, inc=1, device_id=(start + by, me), device_id_type=MESH
                )

    half_rows = pl.ds(row_start, 2 * lt)
    pairs_in = (
        (leaf_in, leaf), (occ_in, occ), (lists_in, lists), (series_in, series),
        (polar_in.at[:, half_rows], polar), (azim_in, azim), (c1_in, c1), (r1_in, r1),
        (ph1_in, ph1), (r2_in.at[half], r2), (c2_in, c2), (ph2_in.at[:, half_rows], ph2),
    )
    copies = [
        pltpu.make_async_copy(source, target, loads.at[i])
        for i, (source, target) in enumerate(pairs_in)
    ]
    for copy in copies:
        copy.start()
    copies[1].wait()
    copies[0].wait()

    w0 = occ[0].astype(jnp.float32) / full_count
    w1 = occ[1].astype(jnp.float32) / full_count
    for r in range(count):
        for c in range(2):
            a = leaf[0, r, c] * w0
            b = leaf[1, r, c] * w1
            mine[r, c] = a + b
            mine[r, 2 + c] = b - a

    pl.semaphore_wait(
        barrier,
        n_dir - 1 + 2 * has_lower.astype(jnp.int32) + 2 * has_upper.astype(jnp.int32),
    )

    def l_copy(r, side, place):
        target = (box if place == 0 else partner) + 2 - 4 * side
        return pltpu.make_async_remote_copy(
            mine.at[r], taken.at[side, r, place], ls.at[side, r, place],
            lr.at[side, r, place], (target, me), device_id_type=MESH,
        )

    for r in range(count):
        for place in range(2):
            @pl.when(has_upper)
            def _():
                l_copy(r, 0, place).start()

            @pl.when(has_lower)
            def _():
                l_copy(r, 1, place).start()

    def d_copy(r, o):
        peer = (me + o) % n_dir
        return pltpu.make_async_remote_copy(
            ready.at[r, peer], out.at[me, r], ds.at[r, o], dr.at[r, n_dir - o],
            (box, peer), device_id_type=MESH,
        )

    def d_arrival(r, o):
        peer = (me + o) % n_dir
        return pltpu.make_async_remote_copy(
            ready.at[r, me], out.at[peer, r], ds.at[r, o], dr.at[r, o],
            (box, peer), device_id_type=MESH,
        )

    ready[...] = jnp.zeros(ready.shape, jnp.float32)
    for copy in copies[2:6]:
        copy.wait()

    slots = lists.shape[1]
    entries = lists.shape[2]
    width = 3 + 2 * (LTR + 1)
    for side in range(2):
        named = jnp.float32(0.0)
        for k in range(entries):
            chosen = lists[pair, 0, k]
            hit = chosen < slots if side == 0 else chosen >= 2 * slots
            named = named + jnp.where(hit, 1.0, 0.0)
        scale = named / entries
        base = side * width

        def oper_step(i, carry):
            rows = pl.ds(pl.multiple_of(i * 8, 8), 8)
            along_x = polar[0, rows] * azim[0:1]
            along_y = polar[0, rows] * azim[1:2]
            along_z = polar[1, rows] * jnp.ones_like(along_x)
            u = (
                series[pair, base] * along_x
                + series[pair, base + 1] * along_y
                + series[pair, base + 2] * along_z
            )
            now, nxt = jnp.ones_like(u), u
            real, imag = jnp.zeros_like(u), jnp.zeros_like(u)
            for degree in range(LTR + 1):
                real = real + series[pair, base + 3 + 2 * degree] * now
                imag = imag + series[pair, base + 4 + 2 * degree] * now
                now, nxt = nxt, (
                    ((2.0 * degree + 3.0) / (degree + 2.0)) * (u * nxt)
                    - ((degree + 1.0) / (degree + 2.0)) * now
                )
            oper[side, 0, rows] = real * scale
            oper[side, 1, rows] = imag * scale
            return carry

        lax.fori_loop(0, 2 * lt // 8, oper_step, 0)

    for copy in copies[6:]:
        copy.wait()

    def first_level(source):
        for k in range(4):
            high, low = split(source[k])
            rows = pl.ds(k * lt, lt)
            lhs1[rows, 0:lp] = high
            lhs1[rows, lp : 2 * lp] = low
            lhs1[rows, 2 * lp : 3 * lp] = high
        stretched = dot(lhs1[...], c1[...])
        for k in range(4):
            high, low = split(stretched[k * lt : (k + 1) * lt])
            columns = pl.ds(k * 2 * lp, 2 * lp)
            rhs1[0:lt, columns] = high
            rhs1[lt : 2 * lt, columns] = low
            rhs1[2 * lt : 3 * lt, columns] = high
        sr, si, dre, dim = [
            dot(r1[...], rhs1[:, k * 2 * lp : (k + 1) * 2 * lp]) for k in range(4)
        ]
        cosine, sine = ph1[0], ph1[1]
        return cosine * sr - sine * dim, cosine * si + sine * dre

    sign = (2 * half - 1).astype(jnp.float32)

    def add_side(r, side, closing):
        for place in range(2):
            l_copy(r, side, place).wait_recv()
            fr, fi = first_level(taken.at[side, r, place])
            if place == 0:
                first[0] = fr
                first[1] = fi
        for k, value in enumerate(
            (first[0] + fr, first[1] + fi, (first[0] - fr) * sign, (first[1] - fi) * sign)
        ):
            high, low = split(value)
            columns = pl.ds(k * 2 * lp, 2 * lp)
            rhs2[0 : 2 * lt, columns] = high
            rhs2[2 * lt : 4 * lt, columns] = low
            rhs2[4 * lt : 6 * lt, columns] = high
        for k in range(4):
            high, low = split(dot(r2[...], rhs2[:, k * 2 * lp : (k + 1) * 2 * lp]))
            rows = pl.ds(k * 2 * lt, 2 * lt)
            lhs2[rows, 0 : 2 * lp] = high
            lhs2[rows, 2 * lp : 4 * lp] = low
            lhs2[rows, 4 * lp : 6 * lp] = high
        wide[...] = dot(lhs2[...], c2[...])
        for o in range(1, n_dir + 1):
            d = (me + o) % n_dir
            offset = pl.multiple_of(d * slab, slab)
            sr, si, dre, dim = [
                wide[pl.ds(k * 2 * lt + offset, slab), :] for k in range(4)
            ]
            rows = pl.ds(offset, slab)
            cosine, sine = ph2[0, rows], ph2[1, rows]
            gr = cosine * sr - sine * dim
            gi = cosine * si + sine * dre
            pr, pi = oper[side, 0, rows], oper[side, 1, rows]
            ready[r, d, 0] += pr * gr - pi * gi
            ready[r, d, 1] += pr * gi + pi * gr
            if o < n_dir:
                @pl.when(closing)
                def _():
                    d_copy(r, o).start()

    def level_step(q, carry):
        r = q // 2
        side = q % 2

        closing = jnp.logical_or(side == 1, jnp.logical_not(has_upper))

        @pl.when(jnp.where(side == 0, has_lower, has_upper))
        def _():
            add_side(r, side, closing)

        @pl.when(side == 1)
        def _():
            out[me, r] = ready[r, me]

        return carry

    lax.fori_loop(0, 2 * count, level_step, 0)

    for r in range(count):
        for o in range(1, n_dir):
            d_arrival(r, o).wait_recv()
            d_copy(r, o).wait_send()
        for place in range(2):
            @pl.when(has_upper)
            def _():
                l_copy(r, 0, place).wait_send()

            @pl.when(has_lower)
            def _():
                l_copy(r, 1, place).wait_send()


def per_device(n_box, n_dir, leaf_patterns, occupancy, pair_lists):
    _, count, _, lt, lp = leaf_patterns.shape
    assert leaf_patterns.shape[0] == 2
    slab = 2 * lt // n_dir
    bf16 = jnp.bfloat16
    first_high, first_low = halves(interp_table(lp, 0.0).T)
    c1 = np.concatenate([first_high, first_high, first_low], axis=0)
    row_high, row_low = halves(interp_table(lt, 0.5))
    r1 = np.concatenate([row_high, row_high, row_low], axis=1)
    row_high, row_low = halves(interp_table(2 * lt, 0.5).reshape(2, 2 * lt, 2 * lt))
    r2 = np.concatenate([row_high, row_high, row_low], axis=2)
    high, low = halves(interp_table(2 * lp, 0.0).T)
    c2 = np.concatenate([high, high, low], axis=0)
    st, _, cp, _ = sines(2 * lt, 2 * lp)
    angle = phase_first * st[:, None] * cp[None]
    ph1 = np.stack([np.cos(angle), np.sin(angle)]).astype(np.float32)
    st, ct, cp, sp = sines(4 * lt, 4 * lp)
    angle = phase_second * st[:, None] * sp[None]
    ph2 = np.stack([np.cos(angle), np.sin(angle)]).astype(np.float32)
    polar = np.stack([st, ct])[:, :, None].astype(np.float32)
    azim = np.stack([cp, sp]).astype(np.float32)
    series = series_table(n_box // 2)
    operands = (
        leaf_patterns, occupancy, pair_lists, series, c1, r1, r2, c2, ph1, ph2, polar, azim
    )
    chunk = (2, slab, 4 * lp)
    f32 = jnp.float32
    rows = 2 * lt
    result = pl.pallas_call(
        functools.partial(kernel, (n_box, n_dir, count, lt, lp, slab)),
        out_shape=jax.ShapeDtypeStruct((n_dir, count) + chunk, f32),
        in_specs=[pl.BlockSpec(memory_space=pltpu.HBM)] * len(operands),
        out_specs=pl.BlockSpec(memory_space=pltpu.VMEM),
        scratch_shapes=[
            pltpu.VMEM(leaf_patterns.shape, f32),
            pltpu.SMEM(occupancy.shape, jnp.int32),
            pltpu.SMEM(pair_lists.shape, jnp.int32),
            pltpu.SMEM(series.shape, f32),
            pltpu.VMEM(c1.shape, bf16),
            pltpu.VMEM(r1.shape, bf16),
            pltpu.VMEM(r2.shape[1:], bf16),
            pltpu.VMEM(c2.shape, bf16),
            pltpu.VMEM(ph1.shape, f32),
            pltpu.VMEM((2, rows, 4 * lp), f32),
            pltpu.VMEM((2, rows, 1), f32),
            pltpu.VMEM(azim.shape, f32),
            pltpu.VMEM((count, 4, lt, lp), f32),
            pltpu.VMEM((2, count, 2, 4, lt, lp), f32),
            pltpu.VMEM((4 * lt, 3 * lp), bf16),
            pltpu.VMEM((3 * lt, 8 * lp), bf16),
            pltpu.VMEM((2, rows, 2 * lp), f32),
            pltpu.VMEM((6 * lt, 8 * lp), bf16),
            pltpu.VMEM((8 * lt, 6 * lp), bf16),
            pltpu.VMEM((8 * lt, 4 * lp), f32),
            pltpu.VMEM((count, n_dir) + chunk, f32),
            pltpu.VMEM((2, 2, rows, 4 * lp), f32),
            pltpu.SemaphoreType.DMA((len(operands),)),
            pltpu.SemaphoreType.DMA((2, count, 2)),
            pltpu.SemaphoreType.DMA((2, count, 2)),
            pltpu.SemaphoreType.DMA((count, n_dir)),
            pltpu.SemaphoreType.DMA((count, n_dir)),
        ],
        compiler_params=pltpu.CompilerParams(
            collective_id=0, has_side_effects=True, vmem_limit_bytes=48 << 20
        ),
    )(*[pltpu.with_memory_space_constraint(jnp.asarray(operand), pltpu.HBM) for operand in operands])
    return result.reshape(1, 1, n_dir * count, *chunk)


def solution(mesh):
    placed = (P("box", "dir", None, None, None), P("box"), P())
    return jax.shard_map(
        functools.partial(per_device, mesh.shape["box"], mesh.shape["dir"]),
        mesh=mesh,
        in_specs=placed,
        out_specs=P("box", None, None, None, "dir", None),
        check_vma=False,
    )
```
